32 devices in a mesh: expert: 4 (over x, core), hidden: 8 (over z, y).
Axes of the slice: x: 2, y: 2, z: 4, core: 2. Of those that a mesh axis runs over, the one named last changes fastest.
Arguments:
- tokens: bfloat16 [128, 6144], P(('expert', 'hidden')), may hold values from -33 to 33
- norm_gain: float32 [6144], replicated, may hold values from 0.1 to 1.9
- gate_weight: bfloat16 [4, 6144, 8192], P('expert', None, 'hidden'), may hold values from -0.078125 to 0.078125
- up_weight: bfloat16 [4, 6144, 8192], P('expert', None, 'hidden'), may hold values from -0.078125 to 0.078125
- down_weight: bfloat16 [4, 8192, 6144], P('expert', 'hidden'), may hold values from -0.09375 to 0.09375
- expert_ids: int32 [128, 2], P('expert'), may hold values from 0 to 3, all different within a row; in each aligned block of 4 rows (0 to 3, 4 to 7, ...) at most 2 rows name the same one
- route_weight: float32 [128, 2], P('expert'), may hold values from 0.2 to 1
Outputs:
- settled_state: bfloat16 [128, 6144], P(('expert', 'hidden'))
The draws below stay inside these ranges and needn't reach their ends.
Inputs may be any that keep to these rules, and one draw needn't show every extreme that they name: `expert_ids`: in each aligned block of 4 rows (the tokens of one device) the two ids of a row differ and no expert is named more than 2 times; some expert is named exactly 2 times.
All inputs are finite; a program needn't handle non-finite values.
Results may differ from the reference program's by a relative error of at most 0.0085.
Values may be sent and summed in bfloat16 or wider, within the bound.
A program may use at most 64 MiB of HBM per device.

```python
import math
import jax
import jax.numpy as jnp
import numpy as np
from jax import lax

D = 6144
FF = 8192
TOK_DEV = 4
ITERS = 2
EXPERTS = 4
CAP = 2
TOKENS = 128
N_HIDDEN = 8


def draw_tokens(key, part):
    noise_key, row_key, column_key = jax.random.split(key, 3)
    row_scale = jnp.exp(jax.random.uniform(row_key, (TOKENS, 1), jnp.float32, math.log(0.25), math.log(2.5)))
    column_scale = jnp.exp(jax.random.uniform(column_key, (1, D), jnp.float32, math.log(0.25), math.log(2.5)))
    base = jnp.clip(jax.random.normal(noise_key, (TOKENS, D), jnp.float32), -4.0, 4.0)
    return (base * row_scale * column_scale).astype(jnp.bfloat16)


def spiked(result, own_key, source, target, shards_of, factor):
    owner, partner = [(jnp.arange(result.shape[axis_at]) // (result.shape[axis_at] // shards_of)).reshape([-1 if axis == axis_at else 1 for axis in range(result.ndim)]) for axis_at in (source, target)]
    chosen = jax.random.permutation(own_key, shards_of)[partner]
    strong = (owner == chosen) | (owner == (partner + shards_of // 2) % shards_of)
    return jnp.where(strong, factor * result, result)


def steps_of(rng, dims, pieces, least, high):
    def one(axis_at, blocks):
        heights = jax.random.uniform(jax.random.fold_in(jax.random.fold_in(rng, 6), axis_at), (blocks,), jnp.float32, least / len(pieces), high / len(pieces))
        return jnp.repeat(jnp.exp(heights), dims[axis_at] // blocks).reshape((-1,) + (1,) * (len(dims) - axis_at - 1))

    gain = one(*pieces[0])
    for cut in pieces[1:]:
        gain = gain * one(*cut)
    return gain


def routed_block(rng, own, number, rows, amount, top, limit, lean):
    sequence = jax.random.permutation(rng, amount)
    packed, usual = portions_of(amount, rows * top, limit, lean, True), portions_of(amount, rows * top, limit, lean, False)
    places = jnp.arange(amount)

    def named(tallies, turn):
        used = int((tallies > 0).sum())
        fixed = max(1, used // 4)
        shifted = fixed + (places - fixed + turn * (used - fixed)) % max(1, amount - fixed)
        return jnp.zeros((amount,), jnp.int32).at[sequence[jnp.where(places < fixed, places, shifted)]].set(jnp.asarray(tallies, jnp.int32))

    tallies = jnp.where(number % 4 == 0, named(packed, number // 4), named(usual, number - number // 4 - 1))
    mixed = jax.random.permutation(jax.random.fold_in(own, 3), amount)
    donor, receiver = mixed[0:amount // 2 * 2:2], mixed[1:amount // 2 * 2:2]
    room = jnp.minimum(tallies[donor] - 1, limit - tallies[receiver]) // 2
    room = jnp.where((donor == sequence[0]) | (receiver == sequence[0]) | (tallies[receiver] == 0), 0, jnp.maximum(room, 0))
    shifted = jax.random.randint(jax.random.fold_in(own, 4), (amount // 2,), 0, 1 << 20) % (room + 1)
    tallies = tallies.at[donor].add(-shifted).at[receiver].add(shifted)
    members = jnp.searchsorted(jnp.cumsum(tallies), jnp.arange(rows * top), side="right").astype(jnp.int32)
    table = members.reshape(top, rows).T
    table = table[jax.random.permutation(jax.random.fold_in(own, 1), rows)]
    turn = jax.random.randint(jax.random.fold_in(own, 2), (rows, 1), 0, top)
    return jnp.take_along_axis(table, (jnp.arange(top)[None, :] + turn) % top, axis=1)


def portions_of(amount, total, most, slope, full):
    portions = [(1 << 20) // math.isqrt(rank ** slope) + 1 for rank in range(1, amount + 1)]
    largest = most if full else min(most, max(-(-total // amount), total * portions[0] // sum(portions)))
    least = 1 if total - largest >= amount - 1 else 0
    holding, rest = [largest] + [least] * (amount - 1), total - largest - least * (amount - 1)
    while rest > 0:
        candidates = [i for i in range(1, amount) if holding[i] < largest] or [i for i in range(1, amount) if holding[i] < most]
        whole, budget = sum([portions[i] for i in candidates]), rest
        for i in candidates:
            more = min(most - holding[i], max(1, budget * portions[i] // whole), rest)
            holding[i] = holding[i] + more
            rest = rest - more
    return np.array(holding)


def scatter_about(key, extent, deviation, bound, cuts=(), held_as=jnp.bfloat16):
    entries = deviation * jax.random.normal(key, extent, jnp.float32)
    if cuts:
        entries = entries * steps_of(key, extent, cuts, -0.22, 0.18)
    return jnp.clip(entries, -bound, bound).astype(held_as)


def bell_draw_with(stream_key, shape, deviation, limit, shards, heavy, held_as=jnp.bfloat16):
    entries = deviation * jax.random.normal(stream_key, shape, jnp.float32)
    if shards:
        entries = entries * steps_of(stream_key, shape, shards, -0.22, 0.18)
    return jnp.clip(spiked(entries, jax.random.fold_in(stream_key, 3), *heavy), -limit, limit).astype(held_as)


def setup_inputs(seed: int = 0) -> dict:
    seeds = jax.random.split(jax.random.key(seed), 8)
    tokens = draw_tokens(jax.random.fold_in(seeds[7], 71), 0)
    norm_gain = jnp.clip(1.0 + 0.18 * jax.random.normal(seeds[1], (D,), jnp.float32), 0.1, 1.9)
    gate_weight = scatter_about(seeds[2], (EXPERTS, D, FF), D ** -0.5, 0.078125, ((0, 4), (2, 8)))
    up_weight = scatter_about(seeds[3], (EXPERTS, D, FF), D ** -0.5, 0.078125, ((0, 4), (2, 8)))
    down_weight = bell_draw_with(seeds[4], (EXPERTS, FF, D), FF ** -0.5, 0.09375, ((0, 4), (1, 8)), (1, 2, 8, 2.0))
    expert_ids_keys = jax.random.split(jax.random.fold_in(seeds[5], 1), TOKENS // TOK_DEV)
    expert_ids_turns = jax.random.permutation(jax.random.fold_in(seeds[5], 3), TOKENS // TOK_DEV)
    expert_ids = jax.vmap(lambda own, number: routed_block(jax.random.fold_in(seeds[5], 2), own, number, TOK_DEV, EXPERTS, 2, CAP, 2))(expert_ids_keys, expert_ids_turns).reshape((TOKENS, 2))
    route_weight = jnp.clip(0.2 + 0.8 * jax.random.uniform(seeds[6], (TOKENS, 2), jnp.float32) ** steps_of(seeds[6], (TOKENS, 2), ((0, 4),), -0.2, 0.2), 0.2, 1.0)
    return dict(tokens=tokens, norm_gain=norm_gain, gate_weight=gate_weight, up_weight=up_weight, down_weight=down_weight, expert_ids=expert_ids, route_weight=route_weight)


EPSILON = 1e-05
NUDGE = 0.5

def rms_norm(values, norm_gain):
    widened = values.astype(jnp.float32)
    mean_square = lax.optimization_barrier(jnp.mean(widened * widened, axis=-1, keepdims=True))
    return (widened * lax.rsqrt(mean_square + EPSILON) * norm_gain).astype(jnp.bfloat16)

def expert_outputs(normed, gate_panel, up_panel, down_panel, chosen):
    inputs = jnp.take(normed, chosen, axis=0)
    gate_value = jnp.dot(inputs, gate_panel, preferred_element_type=jnp.float32)
    up_value = jnp.dot(inputs, up_panel, preferred_element_type=jnp.float32)
    hidden_units = (jax.nn.silu(gate_value) * up_value).astype(jnp.bfloat16)
    unit_block = FF // N_HIDDEN

    def add_block(block_index, total):
        start = (block_index * unit_block).astype(jnp.int32)
        units = lax.dynamic_slice_in_dim(hidden_units, start, unit_block, 1)
        panel = lax.dynamic_slice_in_dim(down_panel, start, unit_block, 0)
        partial_sum = jnp.dot(units, panel, preferred_element_type=jnp.float32).astype(jnp.bfloat16)
        partial_sum = lax.optimization_barrier(partial_sum)
        return total + partial_sum.astype(jnp.float32)
    total = lax.fori_loop(0, N_HIDDEN, add_block, jnp.zeros((chosen.shape[0], D), jnp.float32))
    return total.astype(jnp.bfloat16)

def reference(tokens, norm_gain, gate_weight, up_weight, down_weight, expert_ids, route_weight):
    state = tokens
    token_index = jnp.arange(TOKENS, dtype=jnp.int32)
    for iteration in range(ITERS):
        normed = rms_norm(state, norm_gain)

        def one_expert(expert):
            routed = jnp.any(expert_ids == expert, axis=1)
            order_keys = jnp.where(routed, 0, 1).astype(jnp.int32)
            chosen = jnp.argsort(order_keys, stable=True)[:TOKENS // 2].astype(jnp.int32)
            values = expert_outputs(normed, gate_weight[expert], up_weight[expert], down_weight[expert], chosen)
            return jnp.zeros((TOKENS, D), jnp.bfloat16).at[chosen].set(values)
        outputs = lax.map(one_expert, jnp.arange(EXPERTS, dtype=jnp.int32))
        first = outputs[expert_ids[:, 0], token_index].astype(jnp.float32) * route_weight[:, 0:1]
        second = outputs[expert_ids[:, 1], token_index].astype(jnp.float32) * route_weight[:, 1:2]
        mixed = first + second
        state = (NUDGE * state.astype(jnp.float32) + NUDGE * (tokens.astype(jnp.float32) + mixed)).astype(jnp.bfloat16)
    return state
```

```python
import functools

import jax
import jax.numpy as jnp
from jax import lax
from jax.experimental import pallas as pl
from jax.experimental.pallas import tpu as pltpu
from jax.sharding import PartitionSpec as P

ITERS = 2
EPSILON = 1e-05
NUDGE = 0.5
CHUNKS = 4
LANES = 128
MESH = pl.DeviceIdType.MESH
f32, bf16 = jnp.float32, jnp.bfloat16


class Plan:
    def __init__(self, experts, hidden, tok, width, units):
        self.E, self.H, self.tok, self.D, self.U = experts, hidden, tok, width, units
        self.C = 2
        self.X = experts // self.C
        self.Y = 2
        self.Z = hidden // self.Y
        self.R = self.Z * tok
        self.NB = self.C * self.X * self.Y
        self.K = width // CHUNKS
        self.rows = self.NB * self.R
        self.numbers = {}

    def number(self, key):
        return self.numbers.setdefault(key, len(self.numbers))

    def block(self, rc, rx, ry):
        return (rc * self.X + rx) * self.Y + ry


def all_keys(p):
    for rc in range(p.C):
        for rx in range(p.X):
            if rc or rx:
                p.number(("route", rc, rx))
    for i in range(CHUNKS):
        for d in range(1, p.Z):
            p.number(("z", i, d))
        for b in range(1, p.NB):
            p.number(("blk", i, b))
        p.number(("core", i))
        f, s = (p.X, p.Y) if i % 2 == 0 else (p.Y, p.X)
        for d in range(1, f):
            p.number(("first", i, d))
        for d in range(1, s):
            p.number(("second", i, d))
        for d in range(1, p.Z):
            p.number(("back", i, d))


def tiles(count, body):
    if count == 1:
        body(0)
    else:
        pl.loop(0, count)(body)


def kernel(p, tokens_ref, gain_ref, route_ref, gate_hbm, up_hbm, down_hbm, out_ref,
           wg, wu, wd, xg, n4, z1, asm, acc, hid, route_in, wrow, state, keep, cs, cr,
           fs, fr, held, ss, sr, usum, own, bs, br, wsem, send_sem, recv_sem):
    C, X, Y, Z, R, K, T = p.C, p.X, p.Y, p.Z, p.R, p.K, p.tok
    e, h = lax.axis_index("expert"), lax.axis_index("hidden")
    x, c = e // C, e % C
    z, y = h // Y, h % Y

    def at(rc=0, rx=0, ry=0, rz=0):
        return ((x + rx) % X * C + (c + rc) % C, (z + rz) % Z * Y + (y + ry) % Y)

    loads = []
    for i in range(CHUNKS):
        rows = pl.ds(i * K, K)
        loads.append(pltpu.make_async_copy(gate_hbm.at[0, rows, :], wg.at[rows, :], wsem.at[3 * i]))
        loads.append(pltpu.make_async_copy(up_hbm.at[0, rows, :], wu.at[rows, :], wsem.at[3 * i + 1]))
    for i in range(CHUNKS):
        cols = pl.ds(i * K, K)
        loads.append(pltpu.make_async_copy(down_hbm.at[0, :, cols], wd.at[i], wsem.at[3 * i + 2]))
    for load in loads:
        load.start()

    barrier = pltpu.get_barrier_semaphore()
    partners = [at(rc=rc, rx=rx) for rc in range(C) for rx in range(X) if rc or rx]
    partners += [at(ry=d) for d in range(1, Y)] + [at(rz=d) for d in range(1, Z)]
    for partner in partners:
        pl.semaphore_signal(barrier, inc=1, device_id=partner, device_id_type=MESH)

    state[...] = tokens_ref[...].astype(f32)
    pl.semaphore_wait(barrier, len(partners))

    def copy(key, src, dst, to):
        n = p.number(key)
        return pltpu.make_async_remote_copy(
            src_ref=src, dst_ref=dst, send_sem=send_sem.at[n], recv_sem=recv_sem.at[n],
            device_id=to, device_id_type=MESH)

    def send(sent, *args):
        made = copy(*args)
        made.start()
        sent.append(made)

    def arrived(key, dst):
        copy(key, dst, dst, at(rc=1)).wait_recv()

    routes = []
    for rc in range(C):
        for rx in range(X):
            if rc or rx:
                send(routes, ("route", (-rc) % C, (-rx) % X), route_ref,
                     route_in.at[((-rc) % C) * X + (-rx) % X], at(rc=rc, rx=rx))

    def iteration(it, _):
        first_time = it == 0

        values = state[...]
        mean_square = jnp.sum(values * values, axis=-1, keepdims=True) / p.D
        normed = (values * lax.rsqrt(mean_square + EPSILON) * gain_ref[...]).astype(bf16)
        for i in range(CHUNKS):
            n4[i] = normed[:, i * K:(i + 1) * K]
        sent = []
        for i in range(CHUNKS):
            for d in range(1, Z):
                send(sent, ("z", i, Z - d), n4.at[i], z1.at[i, Z - d], at(rz=d))

        def block_to(i, b_from, rc, rx, ry):
            b, rest = b_from % Y, b_from // Y
            fx, fc = rest % X, rest // X
            there = p.block((fc - rc) % C, (fx - rx) % X, (b - ry) % Y)
            send(sent, ("blk", i, there), xg.at[i, b_from], xg.at[i, there], at(rc, rx, ry))

        def got(i, b):
            arrived(("blk", i, b), xg.at[i, b])

        def level1(i):
            for d in range(1, Z):
                arrived(("z", i, d), z1.at[i, d])
            asm[0:T, :] = n4[i].astype(f32)
            for d in range(1, Z):
                asm[d * T:(d + 1) * T, :] = z1[i, d].astype(f32)
            xg[i, 0] = asm[...].astype(bf16)
            for d in range(1, Y):
                block_to(i, 0, 0, 0, d)
            for d in range(1, X):
                block_to(i, 0, 0, d, 0)
            block_to(i, 0, 1, 0, 0)

        def level2(i):
            if i % 2 == 0:
                for ry in range(1, Y):
                    b = p.block(0, 0, ry)
                    got(i, b)
                    for d in range(1, X):
                        block_to(i, b, 0, d, 0)
                    block_to(i, b, 1, 0, 0)
                for rx in range(1, X):
                    b = p.block(0, rx, 0)
                    got(i, b)
                    block_to(i, b, 1, 0, 0)
            else:
                for rx in range(1, X):
                    b = p.block(0, rx, 0)
                    got(i, b)
                    for d in range(1, Y):
                        block_to(i, b, 0, 0, d)
                    block_to(i, b, 1, 0, 0)
                for ry in range(1, Y):
                    b = p.block(0, 0, ry)
                    got(i, b)
                    block_to(i, b, 1, 0, 0)

        def level3(i):
            for rx in range(1, X):
                for ry in range(1, Y):
                    b = p.block(0, rx, ry)
                    got(i, b)
                    block_to(i, b, 1, 0, 0)

        per = max(1, min(p.NB, 128 // R))
        row_tiles = p.NB // per
        high = per * R
        wide = min(512, p.U)

        def multiply(i):
            for b in range(X * Y, p.NB):
                got(i, b)

            @pl.when(first_time)
            def _():
                loads[2 * i].wait()
                loads[2 * i + 1].wait()

            def column(n):
                cols = pl.ds(pl.multiple_of(n * wide, wide), wide)

                def row(m):
                    block = xg[i, pl.ds(m * per, per)].reshape(high, K)
                    place = pl.ds(pl.multiple_of(m * high, high), high)
                    for side, weight in ((0, wg), (1, wu)):
                        product = jnp.dot(block, weight[pl.ds(i * K, K), cols], preferred_element_type=f32)
                        if i == 0:
                            acc[side, place, cols] = product
                        else:
                            acc[side, place, cols] += product

                tiles(row_tiles, row)

            tiles(p.U // wide, column)

        for t in range(CHUNKS + 3):
            if t < CHUNKS:
                level1(t)
            if 0 <= t - 1 < CHUNKS:
                level2(t - 1)
            if 0 <= t - 2 < CHUNKS:
                level3(t - 2)
            if 0 <= t - 3 < CHUNKS:
                multiply(t - 3)
        for made in sent:
            made.wait_send()

        @pl.when(first_time)
        def _():
            lane = lax.broadcasted_iota(jnp.int32, (T, LANES), 1)
            for rc in range(C):
                for rx in range(X):
                    if rc or rx:
                        arrived(("route", rc, rx), route_in.at[rc * X + rx])
                    for ry in range(Y):
                        for rz in range(Z):
                            _, whose = at(ry=ry, rz=rz)
                            if rc or rx:
                                part = route_in[rc * X + rx, whose]
                            else:
                                part = route_ref[whose]
                            mine = jnp.sum(jnp.where(lane == e, part, 0.0), axis=1, keepdims=True)
                            base = p.block(rc, rx, ry) * R + rz * T
                            wrow[base:base + T, :] = jnp.broadcast_to(mine, (T, LANES))

        def activate(n):
            cols = pl.ds(pl.multiple_of(n * LANES, LANES), LANES)

            def row(m):
                place = pl.ds(pl.multiple_of(m * high, high), high)
                gate = acc[0, place, cols]
                units = gate / (1.0 + jnp.exp(-gate)) * acc[1, place, cols]
                hid[place, cols] = (units * wrow[place, :]).astype(bf16)

            tiles(row_tiles, row)

        tiles(p.U // LANES, activate)

        sent = []
        half = p.rows // C
        narrow = 512 if K % 512 == 0 else LANES

        def down(i):
            @pl.when(first_time)
            def _():
                loads[2 * CHUNKS + i].wait()

            def column(n):
                cols = pl.ds(pl.multiple_of(n * narrow, narrow), narrow)

                def row(m):
                    place = pl.ds(pl.multiple_of(m * 64, 64), 64)
                    other = pl.ds(pl.multiple_of(half + m * 64, 64), 64)
                    cs[i, place, cols] = jnp.dot(hid[other, :], wd[i, :, cols], preferred_element_type=f32).astype(bf16)
                    keep[i % 2, place, cols] = jnp.dot(hid[place, :], wd[i, :, cols], preferred_element_type=f32)

                tiles(half // 64, row)

            tiles(K // narrow, column)
            send(sent, ("core", i), cs.at[i], cr.at[i], at(rc=1))

        def dims(i):
            if i % 2 == 0:
                return X, Y, lambda a, b: a * Y + b, lambda d: at(rx=d), lambda d: at(ry=d)
            return Y, X, lambda a, b: b * Y + a, lambda d: at(ry=d), lambda d: at(rx=d)

        def reduce1(i):
            arrived(("core", i), cr.at[i])
            F, S, place, to_first, _ = dims(i)
            for a in list(range(1, F)) + [0]:
                for b in range(S):
                    rows = pl.ds(place(a, b) * R, R)
                    total = keep[i % 2, rows, :] + cr[i, rows, :].astype(f32)
                    if a:
                        fs[i, (a - 1) * S + b] = total.astype(bf16)
                    else:
                        held[i % 2, b] = total
                if a:
                    send(sent, ("first", i, a), fs.at[i, pl.ds((a - 1) * S, S)],
                         fr.at[i, pl.ds((a - 1) * S, S)], to_first(a))

        def reduce2(i):
            F, S, _, _, to_second = dims(i)
            for a in range(1, F):
                arrived(("first", i, a), fr.at[i, pl.ds((a - 1) * S, S)])
            for b in list(range(1, S)) + [0]:
                total = held[i % 2, b]
                for a in range(1, F):
                    total = total + fr[i, (a - 1) * S + b].astype(f32)
                if b:
                    ss[i, b - 1] = total.astype(bf16)
                    send(sent, ("second", i, b), ss.at[i, b - 1], sr.at[i, b - 1], to_second(b))
                else:
                    usum[i % 2] = total

        def reduce3(i):
            S = dims(i)[1]
            total = usum[i % 2]
            for b in range(1, S):
                arrived(("second", i, b), sr.at[i, b - 1])
                total = total + sr[i, b - 1].astype(f32)
            asm[...] = total
            for d in range(1, Z):
                bs[i, d - 1] = asm[d * T:(d + 1) * T, :].astype(bf16)
                send(sent, ("back", i, d), bs.at[i, d - 1], br.at[i, d - 1], at(rz=d))
            own[i] = asm[0:T, :]

        def settle(i):
            mixed = own[i]
            for d in range(1, Z):
                arrived(("back", i, d), br.at[i, d - 1])
                mixed = mixed + br[i, d - 1].astype(f32)
            cols = pl.ds(i * K, K)
            fresh = (NUDGE * state[:, cols] + NUDGE * (tokens_ref[:, cols].astype(f32) + mixed)).astype(bf16)
            state[:, cols] = fresh.astype(f32)
            out_ref[:, cols] = fresh

        steps = (down, reduce1, reduce2, reduce3, settle)
        for t in range(CHUNKS + len(steps) - 1):
            for lag, step in enumerate(steps):
                if 0 <= t - lag < CHUNKS:
                    step(t - lag)
        for made in sent:
            made.wait_send()
        return 0

    lax.fori_loop(0, ITERS, iteration, 0)
    for made in routes:
        made.wait_send()


def on_device(experts, hidden, tokens, norm_gain, gate_weight, up_weight, down_weight, expert_ids, route_weight):
    tok, width = tokens.shape
    p = Plan(experts, hidden, tok, width, gate_weight.shape[2])
    all_keys(p)
    lanes = jnp.arange(LANES, dtype=jnp.int32)[None, :]
    table = (jnp.where(expert_ids[:, 0:1] == lanes, route_weight[:, 0:1], 0.0)
             + jnp.where(expert_ids[:, 1:2] == lanes, route_weight[:, 1:2], 0.0))
    table = table.reshape(hidden, tok, LANES)
    n, K, R, U = len(p.numbers), p.K, p.R, p.U
    S, FS = max(p.X, p.Y), max((p.X - 1) * p.Y, (p.Y - 1) * p.X)
    half = p.rows // p.C
    vmem = pltpu.VMEM
    scratch = [
        vmem((width, U), bf16), vmem((width, U), bf16), vmem((CHUNKS, U, K), bf16),
        vmem((CHUNKS, p.NB, R, K), bf16),
        vmem((CHUNKS, tok, K), bf16), vmem((CHUNKS, p.Z, tok, K), bf16), vmem((R, K), f32),
        vmem((2, p.rows, U), f32), vmem((p.rows, U), bf16),
        vmem((experts, hidden, tok, LANES), f32), vmem((p.rows, LANES), f32),
        vmem((tok, width), f32),
        vmem((2, half, K), f32), vmem((CHUNKS, half, K), bf16), vmem((CHUNKS, half, K), bf16),
        vmem((CHUNKS, FS, R, K), bf16), vmem((CHUNKS, FS, R, K), bf16),
        vmem((2, S, R, K), f32),
        vmem((CHUNKS, S - 1, R, K), bf16), vmem((CHUNKS, S - 1, R, K), bf16),
        vmem((2, R, K), f32),
        vmem((CHUNKS, tok, K), f32),
        vmem((CHUNKS, p.Z - 1, tok, K), bf16), vmem((CHUNKS, p.Z - 1, tok, K), bf16),
        pltpu.SemaphoreType.DMA((3 * CHUNKS,)),
        pltpu.SemaphoreType.DMA((n,)), pltpu.SemaphoreType.DMA((n,)),
    ]
    inside = pl.BlockSpec(memory_space=pltpu.VMEM)
    outside = pl.BlockSpec(memory_space=pl.ANY)
    return pl.pallas_call(
        functools.partial(kernel, p),
        out_shape=jax.ShapeDtypeStruct((tok, width), bf16),
        in_specs=[inside] * 3 + [outside] * 3,
        out_specs=inside,
        scratch_shapes=scratch,
        compiler_params=pltpu.CompilerParams(
            collective_id=0, has_side_effects=True, vmem_limit_bytes=67_000_000),
        name="settle",
    )(tokens, norm_gain.reshape(1, width), table, gate_weight, up_weight, down_weight)


def solution(mesh):
    placed = (
        P(("expert", "hidden"), None),
        P(),
        P("expert", None, "hidden"),
        P("expert", None, "hidden"),
        P("expert", "hidden", None),
        P("expert", None),
        P("expert", None),
    )
    return jax.shard_map(
        functools.partial(on_device, mesh.shape["expert"], mesh.shape["hidden"]),
        mesh=mesh,
        in_specs=placed,
        out_specs=P(("expert", "hidden"), None),
        check_vma=False,
    )
```

```python
import functools

import jax
import jax.numpy as jnp
from jax import lax
from jax.experimental import pallas as pl
from jax.experimental.pallas import tpu as pltpu
from jax.sharding import PartitionSpec as P

ITERS = 2
EPSILON = 1e-05
NUDGE = 0.5
CHUNKS = 6
LANES = 128
MESH = pl.DeviceIdType.MESH
f32, bf16 = jnp.float32, jnp.bfloat16


class Plan:
    def __init__(self, experts, hidden, tok, width, units):
        self.E, self.H, self.tok, self.D, self.U = experts, hidden, tok, width, units
        self.C = 2
        self.X = experts // self.C
        self.Y = 2
        self.Z = hidden // self.Y
        self.R = self.Z * tok
        self.NB = self.C * self.X * self.Y
        self.K = width // CHUNKS
        self.rows = self.NB * self.R
        self.numbers = {}

    def number(self, key):
        return self.numbers.setdefault(key, len(self.numbers))

    def block(self, rc, rx, ry):
        return (rc * self.X + rx) * self.Y + ry


def all_keys(p):
    for rc in range(p.C):
        for rx in range(p.X):
            if rc or rx:
                p.number(("route", rc, rx))
    for i in range(CHUNKS):
        for d in range(1, p.Z):
            p.number(("z", i, d))
        for b in range(1, p.NB):
            p.number(("blk", i, b))
        p.number(("core", i))
        f, s = (p.X, p.Y) if i % 2 == 0 else (p.Y, p.X)
        for d in range(1, f):
            p.number(("first", i, d))
        for d in range(1, s):
            p.number(("second", i, d))
        for d in range(1, p.Z):
            p.number(("back", i, d))


def tiles(count, body):
    if count == 1:
        body(0)
    else:
        pl.loop(0, count)(body)


def kernel(p, tokens_ref, gain_ref, route_ref, gate_hbm, up_hbm, down_hbm, out_ref,
           wg, wu, wd, xg, n4, z1, asm, acc, hid, route_in, wrow, state, keep, cs, cr,
           fs, fr, held, ss, sr, usum, own, bs, br, scaled, square, wsem, send_sem, recv_sem):
    C, X, Y, Z, R, K, T = p.C, p.X, p.Y, p.Z, p.R, p.K, p.tok
    e, h = lax.axis_index("expert"), lax.axis_index("hidden")
    x, c = e // C, e % C
    z, y = h // Y, h % Y

    def at(rc=0, rx=0, ry=0, rz=0):
        return ((x + rx) % X * C + (c + rc) % C, (z + rz) % Z * Y + (y + ry) % Y)

    loads = []
    for i in range(CHUNKS):
        rows = pl.ds(i * K, K)
        loads.append(pltpu.make_async_copy(gate_hbm.at[0, rows, :], wg.at[rows, :], wsem.at[3 * i]))
        loads.append(pltpu.make_async_copy(up_hbm.at[0, rows, :], wu.at[rows, :], wsem.at[3 * i + 1]))
    for i in range(CHUNKS):
        cols = pl.ds(i * K, K)
        loads.append(pltpu.make_async_copy(down_hbm.at[0, :, cols], wd.at[i], wsem.at[3 * i + 2]))
    for load in loads:
        load.start()

    barrier = pltpu.get_barrier_semaphore()
    partners = [at(rc=rc, rx=rx) for rc in range(C) for rx in range(X) if rc or rx]
    partners += [at(ry=d) for d in range(1, Y)] + [at(rz=d) for d in range(1, Z)]
    for partner in partners:
        pl.semaphore_signal(barrier, inc=1, device_id=partner, device_id_type=MESH)

    state[...] = tokens_ref[...].astype(f32)
    for i in range(CHUNKS):
        n4[i] = tokens_ref[:, i * K:(i + 1) * K]
    pl.semaphore_wait(barrier, len(partners))

    def copy(key, src, dst, to):
        n = p.number(key)
        return pltpu.make_async_remote_copy(
            src_ref=src, dst_ref=dst, send_sem=send_sem.at[n], recv_sem=recv_sem.at[n],
            device_id=to, device_id_type=MESH)

    def send(sent, *args):
        made = copy(*args)
        made.start()
        sent.append(made)

    def arrived(key, dst):
        copy(key, dst, dst, at(rc=1)).wait_recv()

    routes = []
    for rc in range(C):
        for rx in range(X):
            if rc or rx:
                send(routes, ("route", (-rc) % C, (-rx) % X), route_ref,
                     route_in.at[((-rc) % C) * X + (-rx) % X], at(rc=rc, rx=rx))

    gathers, sums = [], []

    def spread(i):
        for d in range(1, Z):
            send(gathers, ("z", i, Z - d), n4.at[i], z1.at[i, Z - d], at(rz=d))

    def settle_sends():
        for made in gathers + sums:
            made.wait_send()
        gathers.clear()
        sums.clear()

    def gather_steps(it):
        def block_to(i, b_from, rc, rx, ry):
            b, rest = b_from % Y, b_from // Y
            fx, fc = rest % X, rest // X
            there = p.block((fc - rc) % C, (fx - rx) % X, (b - ry) % Y)
            send(gathers, ("blk", i, there), xg.at[i, b_from], xg.at[i, there], at(rc, rx, ry))

        def got(i, b):
            arrived(("blk", i, b), xg.at[i, b])

        def level1(i):
            for d in range(1, Z):
                arrived(("z", i, d), z1.at[i, d])
            asm[0:T, :] = n4[i].astype(f32)
            for d in range(1, Z):
                asm[d * T:(d + 1) * T, :] = z1[i, d].astype(f32)
            xg[i, 0] = asm[...].astype(bf16)
            for d in range(1, Y):
                block_to(i, 0, 0, 0, d)
            for d in range(1, X):
                block_to(i, 0, 0, d, 0)
            block_to(i, 0, 1, 0, 0)

        def level2(i):
            if i % 2 == 0:
                for ry in range(1, Y):
                    b = p.block(0, 0, ry)
                    got(i, b)
                    for d in range(1, X):
                        block_to(i, b, 0, d, 0)
                    block_to(i, b, 1, 0, 0)
                for rx in range(1, X):
                    b = p.block(0, rx, 0)
                    got(i, b)
                    block_to(i, b, 1, 0, 0)
            else:
                for rx in range(1, X):
                    b = p.block(0, rx, 0)
                    got(i, b)
                    for d in range(1, Y):
                        block_to(i, b, 0, 0, d)
                    block_to(i, b, 1, 0, 0)
                for ry in range(1, Y):
                    b = p.block(0, 0, ry)
                    got(i, b)
                    block_to(i, b, 1, 0, 0)

        def level3(i):
            for rx in range(1, X):
                for ry in range(1, Y):
                    b = p.block(0, rx, ry)
                    got(i, b)
                    block_to(i, b, 1, 0, 0)

        def multiply(i):
            for b in range(X * Y, p.NB):
                got(i, b)

            if it == 0:
                loads[2 * i].wait()
                loads[2 * i + 1].wait()

            def row(m):
                place = pl.ds(pl.multiple_of(m * high, high), high)

                def prepare(n):
                    cols = pl.ds(pl.multiple_of(n * LANES, LANES), LANES)
                    gains = gain_ref[:, pl.ds(pl.multiple_of(i * K + n * LANES, LANES), LANES)]
                    part = xg[i, pl.ds(m * per, per), :, cols].reshape(high, LANES).astype(f32)
                    scaled[:, cols] = (part * gains).astype(bf16)
                    if i == 0:
                        @pl.when(n == 0)
                        def _():
                            square[place, :] = part * part

                        @pl.when(n > 0)
                        def _():
                            square[place, :] += part * part
                    else:
                        square[place, :] += part * part

                tiles(K // LANES, prepare)

                def column(n):
                    cols = pl.ds(pl.multiple_of(n * wide, wide), wide)
                    for side, weight in ((0, wg), (1, wu)):
                        product = jnp.dot(scaled[...], weight[pl.ds(i * K, K), cols], preferred_element_type=f32)
                        if i == 0:
                            acc[side, place, cols] = product
                        else:
                            acc[side, place, cols] += product

                tiles(p.U // wide, column)

            tiles(row_tiles, row)

        return level1, level2, level3, multiply

    per = max(1, min(p.NB, 128 // R))
    row_tiles = p.NB // per
    high = per * R
    wide = min(512, p.U)

    def read_routes():
        if True:
            lane = lax.broadcasted_iota(jnp.int32, (T, LANES), 1)
            for rc in range(C):
                for rx in range(X):
                    if rc or rx:
                        arrived(("route", rc, rx), route_in.at[rc * X + rx])
                    for ry in range(Y):
                        for rz in range(Z):
                            _, whose = at(ry=ry, rz=rz)
                            if rc or rx:
                                part = route_in[rc * X + rx, whose]
                            else:
                                part = route_ref[whose]
                            mine = jnp.sum(jnp.where(lane == e, part, 0.0), axis=1, keepdims=True)
                            base = p.block(rc, rx, ry) * R + rz * T
                            wrow[base:base + T, :] = jnp.broadcast_to(mine, (T, LANES))

    def activate_all():
        def root(m):
            place = pl.ds(pl.multiple_of(m * high, high), high)
            mean_square = jnp.sum(square[place, :], axis=1, keepdims=True) / p.D
            square[place, :] = jnp.broadcast_to(lax.rsqrt(mean_square + EPSILON), (high, LANES))

        tiles(row_tiles, root)

        def activate(n):
            cols = pl.ds(pl.multiple_of(n * LANES, LANES), LANES)

            def row(m):
                place = pl.ds(pl.multiple_of(m * high, high), high)
                scale = square[place, :]
                gate = acc[0, place, cols] * scale
                units = gate / (1.0 + jnp.exp(-gate)) * (acc[1, place, cols] * scale)
                hid[place, cols] = (units * wrow[place, :]).astype(bf16)

            tiles(row_tiles, row)

        tiles(p.U // LANES, activate)

    def sum_steps(it):
        half = p.rows // C
        narrow = 512 if K % 512 == 0 else LANES

        def down(i):
            if it == 0:
                loads[2 * CHUNKS + i].wait()

            def column(n):
                cols = pl.ds(pl.multiple_of(n * narrow, narrow), narrow)

                def row(m):
                    place = pl.ds(pl.multiple_of(m * 64, 64), 64)
                    other = pl.ds(pl.multiple_of(half + m * 64, 64), 64)
                    cs[i, place, cols] = jnp.dot(hid[other, :], wd[i, :, cols], preferred_element_type=f32).astype(bf16)
                    keep[i % 2, place, cols] = jnp.dot(hid[place, :], wd[i, :, cols], preferred_element_type=f32)

                tiles(half // 64, row)

            tiles(K // narrow, column)
            send(sums, ("core", i), cs.at[i], cr.at[i], at(rc=1))

        def dims(i):
            if i % 2 == 0:
                return X, Y, lambda a, b: a * Y + b, lambda d: at(rx=d), lambda d: at(ry=d)
            return Y, X, lambda a, b: b * Y + a, lambda d: at(ry=d), lambda d: at(rx=d)

        def reduce1(i):
            arrived(("core", i), cr.at[i])
            F, S, place, to_first, _ = dims(i)
            for a in list(range(1, F)) + [0]:
                for b in range(S):
                    rows = pl.ds(place(a, b) * R, R)
                    total = keep[i % 2, rows, :] + cr[i, rows, :].astype(f32)
                    if a:
                        fs[i, (a - 1) * S + b] = total.astype(bf16)
                    else:
                        held[i % 2, b] = total
                if a:
                    send(sums, ("first", i, a), fs.at[i, pl.ds((a - 1) * S, S)],
                         fr.at[i, pl.ds((a - 1) * S, S)], to_first(a))

        def reduce2(i):
            F, S, _, _, to_second = dims(i)
            for a in range(1, F):
                arrived(("first", i, a), fr.at[i, pl.ds((a - 1) * S, S)])
            for b in list(range(1, S)) + [0]:
                total = held[i % 2, b]
                for a in range(1, F):
                    total = total + fr[i, (a - 1) * S + b].astype(f32)
                if b:
                    ss[i, b - 1] = total.astype(bf16)
                    send(sums, ("second", i, b), ss.at[i, b - 1], sr.at[i, b - 1], to_second(b))
                else:
                    usum[i % 2] = total

        def reduce3(i):
            S = dims(i)[1]
            total = usum[i % 2]
            for b in range(1, S):
                arrived(("second", i, b), sr.at[i, b - 1])
                total = total + sr[i, b - 1].astype(f32)
            asm[...] = total
            for d in range(1, Z):
                bs[i, d - 1] = asm[d * T:(d + 1) * T, :].astype(bf16)
                send(sums, ("back", i, d), bs.at[i, d - 1], br.at[i, d - 1], at(rz=d))
            own[i] = asm[0:T, :]

        def settle(i):
            mixed = own[i]
            for d in range(1, Z):
                arrived(("back", i, d), br.at[i, d - 1])
                mixed = mixed + br[i, d - 1].astype(f32)
            cols = pl.ds(i * K, K)
            fresh = (NUDGE * state[:, cols] + NUDGE * (tokens_ref[:, cols].astype(f32) + mixed)).astype(bf16)
            state[:, cols] = fresh.astype(f32)
            if it == ITERS - 1:
                out_ref[:, cols] = fresh
            else:
                n4[i] = fresh
                spread(i)

        return down, reduce1, reduce2, reduce3, settle

    def staggered(steps):
        for t in range(CHUNKS + max(lag for lag, _ in steps)):
            for lag, step in steps:
                if 0 <= t - lag < CHUNKS:
                    step(t - lag)

    for i in range(CHUNKS):
        spread(i)
    staggered(list(enumerate(gather_steps(0))))
    read_routes()
    for it in range(ITERS):
        settle_sends()
        activate_all()
        steps = list(enumerate(sum_steps(it)))
        if it < ITERS - 1:
            steps += [(6 + lag, step) for lag, step in enumerate(gather_steps(it + 1))]
        staggered(steps)
    settle_sends()
    for made in routes:
        made.wait_send()


def on_device(experts, hidden, tokens, norm_gain, gate_weight, up_weight, down_weight, expert_ids, route_weight):
    tok, width = tokens.shape
    p = Plan(experts, hidden, tok, width, gate_weight.shape[2])
    all_keys(p)
    lanes = jnp.arange(LANES, dtype=jnp.int32)[None, :]
    table = jnp.sum(jnp.where(expert_ids[:, :, None] == lanes[None], route_weight[:, :, None], 0.0), axis=1)
    table = table.reshape(hidden, tok, LANES)
    n, K, R, U = len(p.numbers), p.K, p.R, p.U
    S, FS = max(p.X, p.Y), max((p.X - 1) * p.Y, (p.Y - 1) * p.X)
    half = p.rows // p.C
    vmem = pltpu.VMEM
    scratch = [
        vmem((width, U), bf16), vmem((width, U), bf16), vmem((CHUNKS, U, K), bf16),
        vmem((CHUNKS, p.NB, R, K), bf16),
        vmem((CHUNKS, tok, K), bf16), vmem((CHUNKS, p.Z, tok, K), bf16), vmem((R, K), f32),
        vmem((2, p.rows, U), f32), vmem((p.rows, U), bf16),
        vmem((experts, hidden, tok, LANES), f32), vmem((p.rows, LANES), f32),
        vmem((tok, width), f32),
        vmem((2, half, K), f32), vmem((CHUNKS, half, K), bf16), vmem((CHUNKS, half, K), bf16),
        vmem((CHUNKS, FS, R, K), bf16), vmem((CHUNKS, FS, R, K), bf16),
        vmem((2, S, R, K), f32),
        vmem((CHUNKS, S - 1, R, K), bf16), vmem((CHUNKS, S - 1, R, K), bf16),
        vmem((2, R, K), f32),
        vmem((CHUNKS, tok, K), f32),
        vmem((CHUNKS, p.Z - 1, tok, K), bf16), vmem((CHUNKS, p.Z - 1, tok, K), bf16),
        vmem((max(1, min(p.NB, 128 // R)) * R, K), bf16), vmem((p.rows, LANES), f32),
        pltpu.SemaphoreType.DMA((3 * CHUNKS,)),
        pltpu.SemaphoreType.DMA((n,)), pltpu.SemaphoreType.DMA((n,)),
    ]
    inside = pl.BlockSpec(memory_space=pltpu.VMEM)
    outside = pl.BlockSpec(memory_space=pl.ANY)
    return pl.pallas_call(
        functools.partial(kernel, p),
        out_shape=jax.ShapeDtypeStruct((tok, width), bf16),
        in_specs=[inside] * 3 + [outside] * 3,
        out_specs=inside,
        scratch_shapes=scratch,
        compiler_params=pltpu.CompilerParams(
            collective_id=0, has_side_effects=True, vmem_limit_bytes=67_000_000),
        name="settle",
    )(tokens, norm_gain.reshape(1, width), table, gate_weight, up_weight, down_weight)


def solution(mesh):
    placed = (
        P(("expert", "hidden"), None),
        P(),
        P("expert", None, "hidden"),
        P("expert", None, "hidden"),
        P("expert", "hidden", None),
        P("expert", None),
        P("expert", None),
    )
    return jax.shard_map(
        functools.partial(on_device, mesh.shape["expert"], mesh.shape["hidden"]),
        mesh=mesh,
        in_specs=placed,
        out_specs=P(("expert", "hidden"), None),
        check_vma=False,
    )
```
